32 devices in a mesh: grp: 2 (over y), dp: 4 (over x, core), slab: 4 (over z).
Axes of the slice: x: 2, y: 2, z: 4, core: 2. Of those that a mesh axis runs over, the one named last changes fastest.
Arguments:
- feats: bfloat16 [8, 32, 32, 128, 128], P(('grp', 'dp'), None, 'slab'), parts along dimension 0, may hold values from -6 to 6
- grains: int32 [8, 32, 128, 128], P(('grp', 'dp'), 'slab'), parts along dimension 0, may hold values from 0 to 4095
- spec_weight: bfloat16 [256, 16, 2048], P('slab'), may hold values from -0.75 to 0.75
- taps: float32 [27, 32], replicated, may hold values from -1.25 to 1.25
- point_weight: bfloat16 [32, 32], replicated, may hold values from -1 to 1
- bias: float32 [32], replicated, may hold values from -4 to 4
- cotangent: bfloat16 [8, 32, 32, 128, 128], P(('grp', 'dp'), None, 'slab'), parts along dimension 0, may hold values from -3 to 3
Outputs:
- grad_feats: bfloat16 [8, 32, 32, 128, 128], P(('grp', 'dp'), None, 'slab'), parts along dimension 0
- grad_spec: float32 [256, 32, 2048], P('slab', 'grp', 'dp'), parts along dimension 1
The draws below stay inside these ranges and needn't reach their ends.
There are 2 independent parts, one for each index of `grp`. The reference program is written for one: setup_inputs(seed, part) draws one part's arguments, and reference() takes and returns one part's arrays. A program takes and returns all parts, laid end to end along the dimension named above; an argument that names none is the same for every part. Nothing has to cross between parts.
All inputs are finite; a program needn't handle non-finite values.
Results may differ from the reference program's by a relative error of at most 0.017.
Values may be sent and summed in bfloat16 or wider, within the bound.
A program may use at most 192 MiB of HBM per device.

```python
import math
import jax
import jax.numpy as jnp
from jax import lax

C = 32
NX = 128
NY = 128
NZ = 32
KX = 16
KY = 16
KZ = 16
GRAINS = 4096
SAMPLES = 4


def draw_grains(key, part):
    key_table, key_shift_x, key_shift_y = jax.random.split(jax.random.fold_in(key, 11), 3)
    blocks_x = NX // 8 + 1
    blocks_y = NY // 8 + 1
    table = jax.random.randint(key_table, (SAMPLES, NZ, blocks_x, blocks_y), 0, GRAINS, dtype=jnp.int32)
    table = table.at[0, 0, 0, 0].set(GRAINS - 1)
    shift_x = jax.random.randint(key_shift_x, (SAMPLES, NZ, 1, NY), 0, 8, dtype=jnp.int32)
    shift_y = jax.random.randint(key_shift_y, (SAMPLES, NZ, NX, 1), 0, 8, dtype=jnp.int32)
    block_x = (jnp.arange(NX, dtype=jnp.int32)[None, None, :, None] + shift_x) // 8
    block_y = (jnp.arange(NY, dtype=jnp.int32)[None, None, None, :] + shift_y) // 8
    sample_index = jnp.arange(SAMPLES, dtype=jnp.int32)[:, None, None, None]
    plane_index = jnp.arange(NZ, dtype=jnp.int32)[None, :, None, None]
    return table[sample_index, plane_index, block_x, block_y]


def level_of(stream_key, extent, cuts, smallest, top_value):
    gain, own = 1.0, jax.random.fold_in(stream_key, 6)
    for dim, shards_of in cuts:
        draws = jnp.exp(jax.random.uniform(jax.random.fold_in(own, dim), (shards_of,), jnp.float32, smallest / len(cuts), top_value / len(cuts)))
        gain = gain * jnp.repeat(draws, extent[dim] // shards_of).reshape([-1 if axis == dim else 1 for axis in range(len(extent))])
    return gain


def centred(stream_key, dims, scale, most, cuts=(), kind=jnp.bfloat16):
    array = jax.random.normal(stream_key, dims, jnp.float32) * scale
    if len(cuts) > 0:
        array = level_of(stream_key, dims, cuts, -0.22, 0.18) * array
    return jnp.clip(array, min=-most, max=most).astype(kind)


def setup_inputs(seed: int = 0, part: int = 0) -> dict:
    seeds = jax.random.split(jax.random.key(seed), 8)
    part_splits = jax.random.split(jax.random.fold_in(seeds[7], part), 8)
    feats = centred(part_splits[0], (SAMPLES, C, NZ, NX, NY), 1.0, 6.0, ((0, 4), (2, 4)))
    grains = draw_grains(jax.random.fold_in(jax.random.fold_in(seeds[7], part), 71), part)
    spec_weight = centred(seeds[2], (KX * KY, KZ, 2 * C * C), (2 * C) ** -0.5, 0.75, ((0, 4),))
    taps = centred(seeds[3], (27, C), 27 ** -0.5, 1.25, (), jnp.float32)
    point_weight = centred(seeds[4], (C, C), C ** -0.5, 1.0)
    bias = centred(seeds[5], (C,), 1.0, 4.0, (), jnp.float32)
    cotangent = centred(part_splits[6], (SAMPLES, C, NZ, NX, NY), 0.5, 3.0, ((0, 4), (2, 4)))
    return {"feats": feats, "grains": grains, "spec_weight": spec_weight, "taps": taps, "point_weight": point_weight, "bias": bias, "cotangent": cotangent}


HIGHEST = lax.Precision.HIGHEST

def tables(count, length, start, span):
    indices = jnp.arange(count, dtype=jnp.int32)
    frequency = jnp.where(indices < count // 2, indices, length - count + indices)
    position = start + jnp.arange(span, dtype=jnp.int32)
    phases = frequency[:, None] * position[None, :] % length
    angles = phases.astype(jnp.float32) * (2.0 * math.pi / length)
    return (jnp.cos(angles), jnp.sin(angles))

def mobility(grains):
    leading = [(0, 0)] * (grains.ndim - 2)
    along_x = (grains[..., 1:, :] != grains[..., :-1, :]).astype(jnp.float32)
    along_y = (grains[..., :, 1:] != grains[..., :, :-1]).astype(jnp.float32)
    differ = jnp.pad(along_x, leading + [(1, 0), (0, 0)]) + jnp.pad(along_x, leading + [(0, 1), (0, 0)])
    differ = differ + jnp.pad(along_y, leading + [(0, 0), (1, 0)]) + jnp.pad(along_y, leading + [(0, 0), (0, 1)])
    return 0.25 * (1.0 + differ)

def stencil(padded, taps, adjoint):
    planes = padded.shape[-3] - 2
    rows_x = padded.shape[-2] - 2
    rows_y = padded.shape[-1] - 2
    total = jnp.zeros(padded.shape[:-3] + (planes, rows_x, rows_y), jnp.float32)
    for offset in range(27):
        shift_z, shift_x, shift_y = (offset // 9, offset // 3 % 3, offset % 3)
        if adjoint:
            shift_z, shift_x, shift_y = (2 - shift_z, 2 - shift_x, 2 - shift_y)
        window = padded[..., shift_z:shift_z + planes, shift_x:shift_x + rows_x, shift_y:shift_y + rows_y]
        total = total + taps[offset][:, None, None, None] * window.astype(jnp.float32)
    return total

def plane_forward(field, cos_x, sin_x, cos_y, sin_y):
    real_y = jnp.einsum('...xy,ky->...xk', field, cos_y, precision=HIGHEST)
    imag_y = -jnp.einsum('...xy,ky->...xk', field, sin_y, precision=HIGHEST)
    real_part = jnp.einsum('...xk,jx->...jk', real_y, cos_x, precision=HIGHEST) + jnp.einsum('...xk,jx->...jk', imag_y, sin_x, precision=HIGHEST)
    imag_part = jnp.einsum('...xk,jx->...jk', imag_y, cos_x, precision=HIGHEST) - jnp.einsum('...xk,jx->...jk', real_y, sin_x, precision=HIGHEST)
    return (real_part, imag_part)

def plane_inverse(real_part, imag_part, cos_x, sin_x, cos_y, sin_y):
    real_x = jnp.einsum('...jk,jx->...xk', real_part, cos_x, precision=HIGHEST) - jnp.einsum('...jk,jx->...xk', imag_part, sin_x, precision=HIGHEST)
    imag_x = jnp.einsum('...jk,jx->...xk', imag_part, cos_x, precision=HIGHEST) + jnp.einsum('...jk,jx->...xk', real_part, sin_x, precision=HIGHEST)
    return jnp.einsum('...xk,ky->...xy', real_x, cos_y, precision=HIGHEST) - jnp.einsum('...xk,ky->...xy', imag_x, sin_y, precision=HIGHEST)

def reference(feats, grains, spec_weight, taps, point_weight, bias, cotangent):
    cos_x, sin_x = tables(KX, NX, 0, NX)
    cos_y, sin_y = tables(KY, NY, 0, NY)
    cos_z, sin_z = tables(KZ, NZ, 0, NZ)
    cell_scale = math.sqrt(NX * NY * NZ)
    mode_scale = math.sqrt(KX * KY * KZ)
    weights = spec_weight.astype(jnp.float32).reshape(KX * KY, KZ, 2, C, C)
    w_real = weights[:, :, 0]
    w_imag = weights[:, :, 1]
    point_wide = point_weight.astype(jnp.float32)

    def forward_modes(field):
        real_plane, imag_plane = plane_forward(field, cos_x, sin_x, cos_y, sin_y)
        real_modes = jnp.einsum('czjk,lz->cljk', real_plane, cos_z, precision=HIGHEST) + jnp.einsum('czjk,lz->cljk', imag_plane, sin_z, precision=HIGHEST)
        imag_modes = jnp.einsum('czjk,lz->cljk', imag_plane, cos_z, precision=HIGHEST) - jnp.einsum('czjk,lz->cljk', real_plane, sin_z, precision=HIGHEST)
        real_modes = real_modes.transpose(2, 3, 1, 0).reshape(KX * KY, KZ, C)
        imag_modes = imag_modes.transpose(2, 3, 1, 0).reshape(KX * KY, KZ, C)
        return (real_modes, imag_modes)

    def inverse_modes(real_modes, imag_modes):
        real_in = real_modes.reshape(KX, KY, KZ, C).transpose(3, 2, 0, 1)
        imag_in = imag_modes.reshape(KX, KY, KZ, C).transpose(3, 2, 0, 1)
        real_plane = jnp.einsum('cljk,lz->czjk', real_in, cos_z, precision=HIGHEST) - jnp.einsum('cljk,lz->czjk', imag_in, sin_z, precision=HIGHEST)
        imag_plane = jnp.einsum('cljk,lz->czjk', imag_in, cos_z, precision=HIGHEST) + jnp.einsum('cljk,lz->czjk', real_in, sin_z, precision=HIGHEST)
        return plane_inverse(real_plane, imag_plane, cos_x, sin_x, cos_y, sin_y)

    def one_sample(carry, inputs):
        field, sample_grains, sample_cotangent = inputs
        moving = mobility(sample_grains)[None]
        padded = jnp.pad(field, ((0, 0), (1, 1), (1, 1), (1, 1)))
        smooth = stencil(padded, taps, False).astype(jnp.bfloat16)
        local_part = moving * jnp.einsum('czxy,co->ozxy', smooth.astype(jnp.float32), point_wide, precision=HIGHEST)
        spec_real, spec_imag = forward_modes(field.astype(jnp.float32))
        spec_real = spec_real / cell_scale
        spec_imag = spec_imag / cell_scale
        mixed_real = jnp.einsum('pkc,pkco->pko', spec_real, w_real, precision=HIGHEST) - jnp.einsum('pkc,pkco->pko', spec_imag, w_imag, precision=HIGHEST)
        mixed_imag = jnp.einsum('pkc,pkco->pko', spec_real, w_imag, precision=HIGHEST) + jnp.einsum('pkc,pkco->pko', spec_imag, w_real, precision=HIGHEST)
        spectral = inverse_modes(mixed_real, mixed_imag) / mode_scale
        pre = spectral + local_part + bias[:, None, None, None]
        gate = jax.nn.sigmoid(pre)
        delta = (sample_cotangent.astype(jnp.float32) * gate * (1.0 + pre * (1.0 - gate))).astype(jnp.bfloat16)
        dual_real, dual_imag = forward_modes(delta.astype(jnp.float32))
        dual_real = dual_real / mode_scale
        dual_imag = dual_imag / mode_scale
        grad_real = jnp.einsum('pkc,pko->pkco', spec_real, dual_real, precision=HIGHEST) + jnp.einsum('pkc,pko->pkco', spec_imag, dual_imag, precision=HIGHEST)
        grad_imag = jnp.einsum('pkc,pko->pkco', spec_real, dual_imag, precision=HIGHEST) - jnp.einsum('pkc,pko->pkco', spec_imag, dual_real, precision=HIGHEST)
        back_real = jnp.einsum('pko,pkco->pkc', dual_real, w_real, precision=HIGHEST) + jnp.einsum('pko,pkco->pkc', dual_imag, w_imag, precision=HIGHEST)
        back_imag = jnp.einsum('pko,pkco->pkc', dual_imag, w_real, precision=HIGHEST) - jnp.einsum('pko,pkco->pkc', dual_real, w_imag, precision=HIGHEST)
        spectral_back = inverse_modes(back_real, back_imag) / cell_scale
        spread = (moving * jnp.einsum('ozxy,co->czxy', delta.astype(jnp.float32), point_wide, precision=HIGHEST)).astype(jnp.bfloat16)
        local_back = stencil(jnp.pad(spread, ((0, 0), (1, 1), (1, 1), (1, 1))), taps, True)
        grad_field = (spectral_back + local_back).astype(jnp.bfloat16)
        carry = carry + jnp.stack([grad_real, grad_imag], axis=2)
        return (carry, grad_field)
    start = jnp.zeros((KX * KY, KZ, 2, C, C), jnp.float32)
    summed, grad_feats = lax.scan(one_sample, start, (feats, grains, cotangent))
    grad_spec = (summed / SAMPLES).reshape(KX * KY, KZ, 2 * C * C)
    return (grad_feats, grad_spec)
```

```python
import functools
import math

import jax
import jax.numpy as jnp
import numpy as np
from jax import lax
from jax.experimental import pallas as pl
from jax.experimental.pallas import tpu as pltpu
from jax.sharding import PartitionSpec as P

NX = 128
NY = 128
NZ = 32
KX = 16
KY = 16
KZ = 16
F32 = jnp.float32
BF16 = jnp.bfloat16
HIGHEST = lax.Precision.HIGHEST
MIB = 1 << 20


def waves(count, length):
    index = np.arange(count)
    frequency = np.where(index < count // 2, index, length - count + index)
    phases = frequency[:, None] * np.arange(length)[None, :] % length
    angles = phases * (2.0 * math.pi / length)
    return np.cos(angles), np.sin(angles)


class Plan:
    def __init__(self, planes, slabs):
        self.planes = planes
        self.slabs = slabs
        rows = KX * KY // slabs
        self.rows = rows
        self.groups = slabs if rows >= KY else KX
        self.jl = KX // self.groups
        self.kq = slabs // self.groups
        self.kk = KY // self.kq
        self.width = max(128, planes * KY)
        self.used = planes * KY
        self.pk = planes * self.kk
        self.lanes = self.kk * KZ
        self.lead = self.groups if (2 * self.jl) % 8 == 0 else 1
        width, jl = self.width, self.jl
        cos_x, sin_x = waves(KX, NX)
        cos_y, sin_y = waves(KY, NY)
        cos_z, sin_z = waves(KZ, NZ)
        forward = np.zeros((planes, NY, 2, width))
        for z in range(planes):
            forward[z, :, 0, z * KY : (z + 1) * KY] = cos_y.T
            forward[z, :, 1, z * KY : (z + 1) * KY] = -sin_y.T
        forward = forward.reshape(planes * NY, 2 * width)
        self.y_forward = forward
        self.y_inverse = forward.T
        table = np.zeros((self.groups, 2, jl, 2, NX))
        back = np.zeros((2, NX, self.groups, 2, jl))
        for j in range(KX):
            g, i = divmod(j, jl)
            table[g, 0, i, 0], table[g, 0, i, 1] = cos_x[j], sin_x[j]
            table[g, 1, i, 1], table[g, 1, i, 0] = cos_x[j], -sin_x[j]
            back[0, :, g, 0, i], back[0, :, g, 1, i] = cos_x[j], -sin_x[j]
            back[1, :, g, 1, i], back[1, :, g, 0, i] = cos_x[j], sin_x[j]
        self.x_forward = table.reshape(2 * KX, 2 * NX)
        self.x_inverse = back.reshape(2 * NX, 2 * KX)
        kk, pk, lanes = self.kk, self.pk, self.lanes
        zf = np.zeros((slabs, planes, kk, 2, kk, KZ))
        self.pw = max(128, pk)
        zi = np.zeros((slabs, 2, kk, KZ, 2, planes, kk))
        for s in range(slabs):
            for z in range(planes):
                c, n = cos_z[:, s * planes + z], sin_z[:, s * planes + z]
                for k in range(kk):
                    zf[s, z, k, 0, k], zf[s, z, k, 1, k] = c, n
                    zi[s, 0, k, :, 0, z, k], zi[s, 1, k, :, 0, z, k] = c, -n
                    zi[s, 1, k, :, 1, z, k], zi[s, 0, k, :, 1, z, k] = c, n
        self.z_forward = zf.reshape(slabs, pk, 2 * lanes)
        zi = zi.reshape(slabs, 2 * lanes, 2, pk)
        zi = np.pad(zi, ((0, 0), (0, 0), (0, 0), (0, self.pw - pk)))
        self.z_inverse = zi.reshape(slabs, 2 * lanes, 2 * self.pw)


def whole(shape):
    zeros = (0,) * len(shape)
    return pl.BlockSpec(shape, lambda *_: zeros)


def params(mib):
    return pltpu.CompilerParams(vmem_limit_bytes=mib * MIB)


def dot(a, b, **kw):
    return jnp.dot(a, b, preferred_element_type=F32, **kw)


def channel_modes(plan, planes_of, ty, tx):
    field = jnp.concatenate([planes_of(z) for z in range(plan.planes)], axis=1)
    along = dot(field, ty).astype(BF16)
    stacked = jnp.concatenate([along[:, : plan.width], along[:, plan.width :]], axis=0)
    return dot(tx, stacked)


def put_modes(plan, out_ref, c, value):
    if plan.lead == 1:
        out_ref[0, c] = value.astype(BF16)
    else:
        step = 2 * KX // plan.lead
        for g in range(plan.lead):
            out_ref[g, c] = value[g * step : (g + 1) * step].astype(BF16)


def get_modes(plan, ref, c):
    if plan.lead == 1:
        return ref[0, c]
    parts = [ref[g, c].astype(F32) for g in range(plan.lead)]
    return jnp.concatenate(parts, axis=0).astype(BF16)


def planes_kernel(plan, batch, x_ref, ty_ref, tx_ref, out_ref):
    for c in range(batch):
        value = channel_modes(plan, lambda z: x_ref[c, z], ty_ref[...], tx_ref[...])
        put_modes(plan, out_ref, c, value)


def planes_call(plan, field, ty, tx):
    channels, planes = field.shape[:2]
    batch = 4
    step = 2 * KX // plan.lead
    return pl.pallas_call(
        functools.partial(planes_kernel, plan, batch),
        grid=(channels // batch,),
        in_specs=[
            pl.BlockSpec((batch, planes, NX, NY), lambda i: (i, 0, 0, 0)),
            whole(ty.shape),
            whole(tx.shape),
        ],
        out_specs=pl.BlockSpec((plan.lead, batch, step, plan.width), lambda i: (0, i, 0, 0)),
        out_shape=jax.ShapeDtypeStruct((plan.lead, channels, step, plan.width), BF16),
        compiler_params=params(60),
        cost_estimate=pl.CostEstimate(
            flops=2 * channels * NX * planes * NY * 256, bytes_accessed=field.size * 2, transcendentals=0
        ),
        name="plane_modes",
    )(field, ty, tx)


def bands(taps_ref, c, adjoint, group, band_ref):
    row = lax.broadcasted_iota(jnp.int32, (NY, NY), 0)
    col = lax.broadcasted_iota(jnp.int32, (NY, NY), 1)
    diff = row - col
    for dz in range(3):
        for dx in range(3):
            base = 9 * dz + 3 * dx
            t = [taps_ref[base + i, c] for i in range(3)]
            if adjoint:
                t = t[::-1]
            band = jnp.where(
                diff == 0,
                t[1],
                jnp.where(diff == 1, t[2], jnp.where(diff == -1, t[0], 0.0)),
            ).astype(BF16)
            zi, xi = (2 - dz, 2 - dx) if adjoint else (dz, dx)
            for z in range(group):
                band_ref[
                    xi, (z + zi) * NY : (z + zi + 1) * NY, z * NY : (z + 1) * NY
                ] = band


def shifted(plan, x_ref, before_ref, after_ref, c, rows_ref):
    edge = lax.broadcasted_iota(jnp.int32, (NX, NY), 0)
    for i in range(plan.planes + 2):
        if before_ref is None and i in (0, plan.planes + 1):
            continue
        if i == 0:
            plane = before_ref[c]
        elif i == plan.planes + 1:
            plane = after_ref[c]
        else:
            plane = x_ref[c, i - 1]
        wide = plane.astype(F32)
        lower = jnp.where(edge == 0, 0.0, pltpu.roll(wide, 1, 0))
        upper = jnp.where(edge == NX - 1, 0.0, pltpu.roll(wide, NX - 1, 0))
        cols = slice(i * NY, (i + 1) * NY)
        rows_ref[0, :, cols] = lower.astype(BF16)
        rows_ref[1, :, cols] = plane
        rows_ref[2, :, cols] = upper.astype(BF16)


def stencil_kernel(plan, batch, adjoint, group, *refs):
    if adjoint:
        taps_ref, x_ref, out_ref, band_ref, rows_ref = refs
        before_ref = after_ref = None
    else:
        taps_ref, x_ref, before_ref, after_ref, out_ref, band_ref, rows_ref = refs

    @pl.when(pl.program_id(0) == 0)
    def _():
        band_ref[...] = jnp.zeros_like(band_ref)
        rows_ref[...] = jnp.zeros_like(rows_ref)

    first = pl.program_id(0) * batch
    for c in range(batch):
        half = c % 2
        band, rows = band_ref.at[half], rows_ref.at[half]
        bands(taps_ref, first + c, adjoint, group, band)
        shifted(plan, x_ref, before_ref, after_ref, c, rows)
        for z in range(0, plan.planes, group):
            cols = slice(z * NY, (z + group + 2) * NY)
            total = dot(rows[0, :, cols], band[0])
            total = total + dot(rows[1, :, cols], band[1])
            total = total + dot(rows[2, :, cols], band[2])
            for i in range(group):
                out_ref[c, z + i] = total[:, i * NY : (i + 1) * NY].astype(BF16)


def stencil_call(plan, taps, field, rims, adjoint):
    channels, planes = field.shape[:2]
    batch = 4
    group = 2 if planes % 2 == 0 else 1
    specs = [
        pl.BlockSpec(memory_space=pltpu.SMEM),
        pl.BlockSpec((batch, planes, NX, NY), lambda i: (i, 0, 0, 0)),
    ] + [pl.BlockSpec((batch, NX, NY), lambda i: (i, 0, 0))] * len(rims)
    return pl.pallas_call(
        functools.partial(stencil_kernel, plan, batch, adjoint, group),
        grid=(channels // batch,),
        in_specs=specs,
        out_specs=pl.BlockSpec((batch, planes, NX, NY), lambda i: (i, 0, 0, 0)),
        out_shape=jax.ShapeDtypeStruct(field.shape, BF16),
        scratch_shapes=[
            pltpu.VMEM((2, 3, (group + 2) * NY, group * NY), BF16),
            pltpu.VMEM((2, 3, NX, (planes + 2) * NY), BF16),
        ],
        compiler_params=params(60),
        cost_estimate=pl.CostEstimate(
            flops=2 * field.size * 3 * (group + 2) * NY, bytes_accessed=field.size * 4, transcendentals=0
        ),
        name="stencil_back" if adjoint else "stencil",
    )(taps, field, *rims)


def final_kernel(plan, batch, taps_ref, x_ref, before_ref, after_ref, m_ref, tx_ref, ty_ref, out_ref):
    first = pl.program_id(0) * batch
    edge = lax.broadcasted_iota(jnp.int32, (NX, NY), 0)
    diff = lax.broadcasted_iota(jnp.int32, (NY, NY), 0) - lax.broadcasted_iota(jnp.int32, (NY, NY), 1)

    def rim(c, plane, dz):
        wide = plane.astype(F32)
        lower = jnp.where(edge == 0, 0.0, pltpu.roll(wide, 1, 0)).astype(BF16)
        upper = jnp.where(edge == NX - 1, 0.0, pltpu.roll(wide, NX - 1, 0)).astype(BF16)
        band = []
        for dx in (2, 1, 0):
            t = [taps_ref[9 * dz + 3 * dx + i, first + c] for i in range(3)]
            band.append(jnp.where(
                diff == 0,
                t[1],
                jnp.where(diff == 1, t[0], jnp.where(diff == -1, t[2], 0.0)),
            ).astype(BF16))
        return dot(jnp.concatenate([lower, plane, upper], axis=1), jnp.concatenate(band, axis=0))

    for c in range(batch):
        wave = dot(tx_ref[...], get_modes(plan, m_ref, c)).astype(BF16)
        wave = jnp.concatenate([wave[:NX], wave[NX:]], axis=1)
        full = dot(wave, ty_ref[...])
        for z in range(plan.planes):
            total = full[:, z * NY : (z + 1) * NY] + x_ref[c, z].astype(F32)
            if z == 0:
                total = total + rim(c, before_ref[c], 2)
            if z == plan.planes - 1:
                total = total + rim(c, after_ref[c], 0)
            out_ref[c, z] = total.astype(BF16)


def final_call(plan, taps, partial, before, after, modes, tx, ty):
    channels, planes = partial.shape[:2]
    batch = 4
    block = pl.BlockSpec((batch, planes, NX, NY), lambda i: (i, 0, 0, 0))
    rim = pl.BlockSpec((batch, NX, NY), lambda i: (i, 0, 0))
    return pl.pallas_call(
        functools.partial(final_kernel, plan, batch),
        grid=(channels // batch,),
        in_specs=[
            pl.BlockSpec(memory_space=pltpu.SMEM),
            block,
            rim,
            rim,
            pl.BlockSpec((modes.shape[0], batch) + modes.shape[2:], lambda i: (0, i, 0, 0)),
            whole(tx.shape),
            whole(ty.shape),
        ],
        out_specs=block,
        out_shape=jax.ShapeDtypeStruct(partial.shape, BF16),
        compiler_params=params(60),
        cost_estimate=pl.CostEstimate(
            flops=2 * partial.size * 512, bytes_accessed=partial.size * 4, transcendentals=0
        ),
        name="final",
    )(taps, partial, before, after, modes, tx, ty)


def mix_kernel(plan, channels, adjoint, scale_in, scale_out, r_ref, zf_ref, zi_ref, w_ref,
               out_ref, turned_ref, z_scr, s_scr, m_scr, o_scr):
    jl, lanes, pk, pw = plan.jl, plan.lanes, plan.pk, plan.pw
    chunks = 2 * lanes // 128
    total = None
    for s in range(plan.slabs):
        part = dot(r_ref[s].astype(F32), zf_ref[s], precision=HIGHEST)
        total = part if total is None else total + part
    total = total * scale_in
    for q in range(chunks):
        z_scr[q] = total[:, q * 128 : (q + 1) * 128]

    def rows_of(start):
        return jnp.concatenate(
            [z_scr[q, pl.ds(start, channels, stride=2 * jl), :] for q in range(chunks)], axis=1)

    for j in range(jl):
        re, im = rows_of(j), rows_of(jl + j)
        real = re[:, :lanes] + im[:, lanes:]
        imag = im[:, :lanes] - re[:, lanes:]
        s_scr[j, 0] = real
        s_scr[j, 1] = imag
        both = jnp.concatenate([real, imag], axis=0)
        turned_ref[j * lanes : (j + 1) * lanes, :] = both.T.astype(BF16)
        cols = slice(j * lanes, (j + 1) * lanes)
        rows = slice(j * channels, (j + 1) * channels)
        if adjoint:
            for c in range(channels):
                wr = w_ref[0, c, :, cols].astype(F32)
                wi = w_ref[1, c, :, cols].astype(F32)
                br = jnp.sum(wr * real + wi * imag, axis=0, keepdims=True)
                bi = jnp.sum(wr * imag - wi * real, axis=0, keepdims=True)
                m_scr[j * channels + c : j * channels + c + 1, :lanes] = br
                m_scr[j * channels + c : j * channels + c + 1, lanes:] = bi
        else:
            mr = jnp.zeros((channels, lanes), F32)
            mi = jnp.zeros((channels, lanes), F32)
            for c in range(channels):
                wr = w_ref[0, c, :, cols].astype(F32)
                wi = w_ref[1, c, :, cols].astype(F32)
                sr = s_scr[j, 0, c : c + 1, :]
                si = s_scr[j, 1, c : c + 1, :]
                mr = mr + (sr * wr - si * wi)
                mi = mi + (sr * wi + si * wr)
            m_scr[rows, :lanes] = mr
            m_scr[rows, lanes:] = mi
    mixed = m_scr[...] * scale_out
    for s in range(plan.slabs):
        planar = dot(mixed, zi_ref[s], precision=HIGHEST)
        for j in range(jl):
            for part in range(2):
                o_scr[pl.ds(part * jl + j, channels, stride=2 * jl), :] = planar[
                    j * channels : (j + 1) * channels, part * pw : (part + 1) * pw
                ]
        out_ref[s] = o_scr[:, :pk].astype(BF16)


def mix_call(plan, received, weights, zf, zi, adjoint, scale_in, scale_out):
    channels = weights.shape[1]
    rows = channels * 2 * plan.jl
    modes = plan.jl * plan.lanes
    return pl.pallas_call(
        functools.partial(mix_kernel, plan, channels, adjoint, scale_in, scale_out),
        out_shape=(
            jax.ShapeDtypeStruct((plan.slabs, rows, plan.pk), BF16),
            jax.ShapeDtypeStruct((modes, 2 * channels), BF16),
        ),
        scratch_shapes=[
            pltpu.VMEM((2 * plan.lanes // 128, rows, 128), F32),
            pltpu.VMEM((plan.jl, 2, channels, plan.lanes), F32),
            pltpu.VMEM((plan.jl * channels, 2 * plan.lanes), F32),
            pltpu.VMEM((rows, plan.pw), F32),
        ],
        compiler_params=params(60),
        name="mix_back" if adjoint else "mix",
    )(received, zf, zi, weights)


def middle_kernel(plan, channels, g_ref, sm_ref, cot_ref, m_ref, bias_ref, pw_ref, pt_ref,
                  txi_ref, tyi_ref, ty_ref, tx_ref,
                  spread_ref, first_ref, last_ref, modes_ref, wave_scr, delta_scr, move_scr, kp_ref, kt_ref):
    z = pl.program_id(0)
    planes = plan.planes
    width = plan.width

    @pl.when(z == 0)
    def _():
        def body(c, carry):
            wave = dot(txi_ref[...], get_modes(plan, m_ref, c)).astype(BF16)
            wave_scr[c, :, :width] = wave[:NX]
            wave_scr[c, :, width:] = wave[NX:]
            return carry
        lax.fori_loop(0, channels, body, 0, unroll=4)
        rows = channels * 16
        pick = lax.broadcasted_iota(jnp.int32, (rows, channels), 0) >> 4
        pick = pick == lax.broadcasted_iota(jnp.int32, (rows, channels), 1)
        pick = jnp.where(pick, 1.0, 0.0).astype(BF16)
        same = lax.broadcasted_iota(jnp.int32, (rows, rows), 0) & 15
        same = same == (lax.broadcasted_iota(jnp.int32, (rows, rows), 1) & 15)
        for src, dst in ((pt_ref, kp_ref), (pw_ref, kt_ref)):
            tall = dot(pick, src[...]).astype(BF16)
            full = lax.dot_general(tall, pick, (((1,), (1,)), ((), ())), preferred_element_type=F32)
            dst[...] = jnp.where(same, full, 0.0).astype(BF16)

    g = g_ref[0]
    row = lax.broadcasted_iota(jnp.int32, (NX, NY), 0)
    col = lax.broadcasted_iota(jnp.int32, (NX, NY), 1)

    def differs(shift, axis, inside):
        return jnp.where((g != pltpu.roll(g, shift, axis)) & inside, 0.25, 0.0)

    move_scr[...] = (
        0.25
        + differs(1, 0, row > 0)
        + differs(NX - 1, 0, row < NX - 1)
        + differs(1, 1, col > 0)
        + differs(NY - 1, 1, col < NY - 1)
    )
    height = channels * 16
    bias = bias_ref[...]

    def body(pair, carry):
        starts = [pair * 32 + 16 * i for i in range(2)]

        def tile(ref):
            return [ref[:, 0, pl.ds(x, 16), :].reshape(height, NY) for x in starts]

        mixed = dot(kp_ref[...], jnp.concatenate(tile(sm_ref), axis=1))
        cot = tile(cot_ref)
        deltas = []
        for i, x in enumerate(starts):
            moving = move_scr[pl.ds(x, 16), :]
            wave = wave_scr[:, pl.ds(x, 16), :].reshape(height, 2 * width)
            spectral = dot(wave, tyi_ref[...])
            local = mixed[:, i * NY : (i + 1) * NY].reshape(channels, 16, NY) * moving[None]
            pre = spectral.reshape(channels, 16, NY) + local + bias
            gate = 0.5 + 0.5 * jnp.tanh(0.5 * pre)
            delta = cot[i].astype(F32).reshape(channels, 16, NY) * gate * (1.0 + pre * (1.0 - gate))
            delta = delta.astype(BF16)
            delta_scr[:, z, pl.ds(x, 16), :] = delta
            deltas.append(delta.reshape(height, NY))
        turned = dot(kt_ref[...], jnp.concatenate(deltas, axis=1))
        for i, x in enumerate(starts):
            moving = move_scr[pl.ds(x, 16), :]
            value = turned[:, i * NY : (i + 1) * NY].reshape(channels, 16, NY) * moving[None]
            spread_ref[:, 0, pl.ds(x, 16), :] = value.astype(BF16)
        return carry

    for pair in range(NX // 32):
        body(pair, 0)

    @pl.when(z == 0)
    def _():
        first_ref[...] = spread_ref[:, 0]

    @pl.when(z == planes - 1)
    def _():
        last_ref[...] = spread_ref[:, 0]

        def body(i, carry):
            for c in (2 * i, 2 * i + 1):
                value = channel_modes(plan, lambda p: delta_scr[c, p], ty_ref[...], tx_ref[...])
                put_modes(plan, modes_ref, c, value)
            return carry

        lax.fori_loop(0, channels // 2, body, 0)


def middle_call(plan, grains, smooth, cotangent, modes, bias, kp, kt, txi, tyi, ty, tx):
    channels, planes = smooth.shape[:2]
    width = plan.width
    block = pl.BlockSpec((channels, 1, NX, NY), lambda z: (0, z, 0, 0))
    rim = jax.ShapeDtypeStruct((channels, NX, NY), BF16)
    return pl.pallas_call(
        functools.partial(middle_kernel, plan, channels),
        grid=(planes,),
        in_specs=[
            pl.BlockSpec((1, NX, NY), lambda z: (z, 0, 0)),
            block,
            block,
            whole(modes.shape),
            whole((channels, 1, 1)),
            whole(kp.shape),
            whole(kt.shape),
            whole(txi.shape),
            pl.BlockSpec((2 * width, NY), lambda z: (0, z)),
            whole(ty.shape),
            whole(tx.shape),
        ],
        out_specs=[block, whole(rim.shape), whole(rim.shape), whole(modes.shape)],
        out_shape=[jax.ShapeDtypeStruct(smooth.shape, BF16), rim, rim,
                   jax.ShapeDtypeStruct(modes.shape, BF16)],
        scratch_shapes=[
            pltpu.VMEM((channels, NX, 2 * width), BF16),
            pltpu.VMEM((channels, planes, NX, NY), BF16),
            pltpu.VMEM((NX, NY), F32),
            pltpu.VMEM((16 * channels, 16 * channels), BF16),
            pltpu.VMEM((16 * channels, 16 * channels), BF16),
        ],
        compiler_params=params(60),
        name="middle",
    )(grains, smooth, cotangent, modes, bias.reshape(channels, 1, 1), kp, kt, txi, tyi, ty, tx)


def grad_kernel(samples, both_ref, e_ref, out_ref):
    total = None
    for i in range(samples):
        half = both_ref.shape[-1] // 2
        spec, dual = both_ref[i, :, :half], both_ref[i, :, half:]
        term = dot(spec, e_ref[0]) * dot(dual, e_ref[1]) + dot(spec, e_ref[2]) * dot(dual, e_ref[3])
        total = term if total is None else total + term
    out_ref[...] = total


def grad_call(both, pick):
    samples, modes, width = both.shape
    columns = pick.shape[-1]
    batch = min(256, modes)
    return pl.pallas_call(
        functools.partial(grad_kernel, samples),
        grid=(modes // batch,),
        in_specs=[
            pl.BlockSpec((samples, batch, width), lambda i: (0, i, 0)),
            whole(pick.shape),
        ],
        out_specs=pl.BlockSpec((batch, columns), lambda i: (i, 0)),
        out_shape=jax.ShapeDtypeStruct((modes, columns), F32),
        compiler_params=params(60),
        cost_estimate=pl.CostEstimate(
            flops=8 * samples * modes * width * columns, bytes_accessed=modes * columns * 4, transcendentals=0
        ),
        name="grad_modes",
    )(both, pick)


def column_picks(channels, columns):
    column = lax.axis_index("dp") * columns + jnp.arange(columns)
    part = column // (channels * channels)
    c = column // channels % channels
    o = column % channels
    index = jnp.arange(2 * channels)[:, None]
    spec_real = (index == c).astype(F32)
    spec_imag = (index == channels + c).astype(F32) * jnp.where(part == 0, 1.0, -1.0)
    dual_same = (index == part * channels + o).astype(F32)
    dual_other = (index == (1 - part) * channels + o).astype(F32)
    return jnp.stack([spec_real, dual_same, spec_imag, dual_other]).astype(BF16)


def local(feats, grains, spec_weight, taps, point_weight, bias, cotangent):
    samples_here, channels, planes = feats.shape[:3]
    assert samples_here == 1
    slabs = lax.axis_size("slab")
    dp = lax.axis_size("dp")
    plan = Plan(planes, slabs)
    mode_rows = spec_weight.shape[0]
    half = lambda t: jnp.asarray(t.astype(jnp.bfloat16))
    ty, tx = half(plan.y_forward), half(plan.x_forward)
    tyi, txi = half(plan.y_inverse), half(plan.x_inverse)
    zf = jnp.asarray(plan.z_forward.astype(np.float32))
    zi = jnp.asarray(plan.z_inverse.astype(np.float32))
    cell_scale = 1.0 / math.sqrt(NX * NY * NZ)
    mode_scale = 1.0 / math.sqrt(KX * KY * KZ)
    jl, kq, kk, groups = plan.jl, plan.kq, plan.kk, plan.groups

    def swap(value):
        return lax.all_to_all(value, "slab", split_axis=0, concat_axis=0, tiled=True)

    def scatter_modes(modes):
        if plan.lead == 1 or kq > 1 or plan.used < plan.width:
            modes = modes[..., : plan.used].reshape(plan.lead, channels, -1, 2 * jl, planes, kq, kk)
            modes = modes.transpose(0, 2, 5, 1, 3, 4, 6)
        return swap(modes.reshape(slabs, channels * 2 * jl, plan.pk))

    def gather_planes(planar):
        planar = swap(planar)
        if plan.lead == 1 or kq > 1 or plan.used < plan.width:
            planar = planar.reshape(plan.lead, groups // plan.lead, kq, channels, 2 * jl, planes, kk)
            planar = planar.transpose(0, 3, 1, 4, 5, 2, 6).reshape(
                plan.lead, channels, 2 * KX // plan.lead, plan.used)
            return jnp.pad(planar, ((0, 0), (0, 0), (0, 0), (0, plan.width - plan.used)))
        return planar.reshape(plan.lead, channels, 2 * KX // plan.lead, plan.width)

    up = [(i, i + 1) for i in range(slabs - 1)]
    down = [(j, i) for i, j in up]
    field = feats[0]
    before = lax.ppermute(field[:, planes - 1], "slab", up)
    after = lax.ppermute(field[:, 0], "slab", down)
    weights = spec_weight.reshape(mode_rows * KZ, 2 * channels * channels).T
    weights = weights.reshape(2, channels, channels, mode_rows * KZ)
    kp, kt = point_weight, point_weight.T

    received = scatter_modes(planes_call(plan, field, ty, tx))
    mixed, spec = mix_call(plan, received, weights, zf, zi, False, cell_scale, mode_scale)
    modes = gather_planes(mixed)
    smooth = stencil_call(plan, taps, field, (before, after), False)
    spread, first, last, dual_modes = middle_call(
        plan, grains[0], smooth, cotangent[0], modes, bias, kp, kt, txi, tyi, ty, tx)
    spread_before = lax.ppermute(last, "slab", up)
    spread_after = lax.ppermute(first, "slab", down)
    received = scatter_modes(dual_modes)
    partial = stencil_call(plan, taps, spread, (), True)
    back, dual = mix_call(plan, received, weights, zf, zi, True, mode_scale, cell_scale)
    back_modes = gather_planes(back)
    both = jnp.concatenate([spec, dual], axis=1)
    both = lax.all_to_all(
        jnp.broadcast_to(both[None], (dp,) + both.shape), "dp", split_axis=0, concat_axis=0, tiled=True)
    columns = 2 * channels * channels // dp
    pick = column_picks(channels, columns)
    scale = 1.0 / (samples_here * dp)
    grad_spec = grad_call(both, pick * jnp.array([scale, 1, scale, 1], BF16)[:, None, None])
    grad_feats = final_call(plan, taps, partial, spread_before, spread_after, back_modes, txi, tyi)
    return grad_feats[None], grad_spec.reshape(mode_rows, KZ, columns)


def solution(mesh):
    in_specs = (
        P(("grp", "dp"), None, "slab", None, None),
        P(("grp", "dp"), "slab", None, None),
        P("slab", None, None),
        P(),
        P(),
        P(),
        P(("grp", "dp"), None, "slab", None, None),
    )
    out_specs = (P(("grp", "dp"), None, "slab", None, None), P("slab", "grp", "dp"))
    return jax.shard_map(local, mesh=mesh, in_specs=in_specs, out_specs=out_specs, check_vma=False)
```

```python
import functools
import math

import jax
import jax.numpy as jnp
import numpy as np
from jax import lax
from jax.experimental import pallas as pl
from jax.experimental.pallas import tpu as pltpu
from jax.sharding import PartitionSpec as P

NX = 128
NY = 128
NZ = 32
KX = 16
KY = 16
KZ = 16
F32 = jnp.float32
BF16 = jnp.bfloat16
HIGHEST = lax.Precision.HIGHEST
MIB = 1 << 20


def waves(count, length):
    index = np.arange(count)
    frequency = np.where(index < count // 2, index, length - count + index)
    phases = frequency[:, None] * np.arange(length)[None, :] % length
    angles = phases * (2.0 * math.pi / length)
    return np.cos(angles), np.sin(angles)


class Plan:
    def __init__(self, planes, slabs):
        self.planes = planes
        self.slabs = slabs
        rows = KX * KY // slabs
        self.rows = rows
        self.groups = slabs if rows >= KY else KX
        self.jl = KX // self.groups
        self.kq = slabs // self.groups
        self.kk = KY // self.kq
        self.width = max(128, planes * KY)
        self.used = planes * KY
        self.pk = planes * self.kk
        self.lanes = self.kk * KZ
        self.lead = self.groups if (2 * self.jl) % 8 == 0 else 1
        width, jl = self.width, self.jl
        cos_x, sin_x = waves(KX, NX)
        cos_y, sin_y = waves(KY, NY)
        cos_z, sin_z = waves(KZ, NZ)
        forward = np.zeros((planes, NY, 2, width))
        for z in range(planes):
            forward[z, :, 0, z * KY : (z + 1) * KY] = cos_y.T
            forward[z, :, 1, z * KY : (z + 1) * KY] = -sin_y.T
        forward = forward.reshape(planes * NY, 2 * width)
        self.y_forward = forward
        self.y_inverse = forward.T
        table = np.zeros((self.groups, 2, jl, 2, NX))
        back = np.zeros((2, NX, self.groups, 2, jl))
        for j in range(KX):
            g, i = divmod(j, jl)
            table[g, 0, i, 0], table[g, 0, i, 1] = cos_x[j], sin_x[j]
            table[g, 1, i, 1], table[g, 1, i, 0] = cos_x[j], -sin_x[j]
            back[0, :, g, 0, i], back[0, :, g, 1, i] = cos_x[j], -sin_x[j]
            back[1, :, g, 1, i], back[1, :, g, 0, i] = cos_x[j], sin_x[j]
        self.x_forward = table.reshape(2 * KX, 2 * NX)
        self.x_inverse = back.reshape(2 * NX, 2 * KX)
        kk, pk, lanes = self.kk, self.pk, self.lanes
        zf = np.zeros((slabs, planes, kk, 2, kk, KZ))
        self.pw = max(128, pk)
        zi = np.zeros((slabs, 2, kk, KZ, 2, planes, kk))
        for s in range(slabs):
            for z in range(planes):
                c, n = cos_z[:, s * planes + z], sin_z[:, s * planes + z]
                for k in range(kk):
                    zf[s, z, k, 0, k], zf[s, z, k, 1, k] = c, n
                    zi[s, 0, k, :, 0, z, k], zi[s, 1, k, :, 0, z, k] = c, -n
                    zi[s, 1, k, :, 1, z, k], zi[s, 0, k, :, 1, z, k] = c, n
        self.z_forward = zf.reshape(slabs, pk, 2 * lanes)
        zi = zi.reshape(slabs, 2 * lanes, 2, pk)
        zi = np.pad(zi, ((0, 0), (0, 0), (0, 0), (0, self.pw - pk)))
        self.z_inverse = zi.reshape(slabs, 2 * lanes, 2 * self.pw)


def whole(shape):
    zeros = (0,) * len(shape)
    return pl.BlockSpec(shape, lambda *_: zeros)


def params(mib):
    return pltpu.CompilerParams(vmem_limit_bytes=mib * MIB)


def dot(a, b, **kw):
    return jnp.dot(a, b, preferred_element_type=F32, **kw)


def channel_modes(plan, planes_of, ty, tx):
    field = jnp.concatenate([planes_of(z) for z in range(plan.planes)], axis=1)
    along = dot(field, ty).astype(BF16)
    stacked = jnp.concatenate([along[:, : plan.width], along[:, plan.width :]], axis=0)
    return dot(tx, stacked)


def put_modes(plan, out_ref, c, value):
    if plan.lead == 1:
        out_ref[0, c] = value.astype(BF16)
    else:
        step = 2 * KX // plan.lead
        for g in range(plan.lead):
            out_ref[g, c] = value[g * step : (g + 1) * step].astype(BF16)


def get_modes(plan, ref, c):
    if plan.lead == 1:
        return ref[0, c]
    parts = [ref[g, c].astype(F32) for g in range(plan.lead)]
    return jnp.concatenate(parts, axis=0).astype(BF16)


def planes_kernel(plan, batch, x_ref, ty_ref, tx_ref, out_ref):
    for c in range(batch):
        value = channel_modes(plan, lambda z: x_ref[c, z], ty_ref[...], tx_ref[...])
        put_modes(plan, out_ref, c, value)


def planes_call(plan, field, ty, tx):
    channels, planes = field.shape[:2]
    batch = 4
    step = 2 * KX // plan.lead
    return pl.pallas_call(
        functools.partial(planes_kernel, plan, batch),
        grid=(channels // batch,),
        in_specs=[
            pl.BlockSpec((batch, planes, NX, NY), lambda i: (i, 0, 0, 0)),
            whole(ty.shape),
            whole(tx.shape),
        ],
        out_specs=pl.BlockSpec((plan.lead, batch, step, plan.width), lambda i: (0, i, 0, 0)),
        out_shape=jax.ShapeDtypeStruct((plan.lead, channels, step, plan.width), BF16),
        compiler_params=params(60),
        cost_estimate=pl.CostEstimate(
            flops=2 * channels * NX * planes * NY * 256, bytes_accessed=field.size * 2, transcendentals=0
        ),
        name="plane_modes",
    )(field, ty, tx)


def rims_kernel(low_ref, high_ref, first_ref, last_ref):
    first_ref[...] = low_ref[:, 0]
    last_ref[...] = high_ref[:, 0]


def rims_call(field):
    channels, planes = field.shape[:2]
    batch = 8
    rim = pl.BlockSpec((batch, NX, NY), lambda i: (i, 0, 0))
    shape = jax.ShapeDtypeStruct((channels, NX, NY), field.dtype)
    return pl.pallas_call(
        rims_kernel,
        grid=(channels // batch,),
        in_specs=[
            pl.BlockSpec((batch, 1, NX, NY), lambda i: (i, 0, 0, 0)),
            pl.BlockSpec((batch, 1, NX, NY), lambda i: (i, planes - 1, 0, 0)),
        ],
        out_specs=[rim, rim],
        out_shape=[shape, shape],
        compiler_params=params(60),
        name="rims",
    )(field, field)


def bands(taps_ref, c, adjoint, group, band_ref):
    row = lax.broadcasted_iota(jnp.int32, (NY, NY), 0)
    col = lax.broadcasted_iota(jnp.int32, (NY, NY), 1)
    diff = row - col
    for dz in range(3):
        for dx in range(3):
            base = 9 * dz + 3 * dx
            t = [taps_ref[base + i, c] for i in range(3)]
            if adjoint:
                t = t[::-1]
            band = jnp.where(
                diff == 0,
                t[1],
                jnp.where(diff == 1, t[2], jnp.where(diff == -1, t[0], 0.0)),
            ).astype(BF16)
            zi, xi = (2 - dz, 2 - dx) if adjoint else (dz, dx)
            for z in range(group):
                top = (xi * (group + 2) + z + zi) * NY
                band_ref[top : top + NY, z * NY : (z + 1) * NY] = band


def shifted(plan, x_ref, before_ref, after_ref, c, rows_ref):
    edge = lax.broadcasted_iota(jnp.int32, (NX, NY), 0)
    for i in range(plan.planes + 2):
        if before_ref is None and i in (0, plan.planes + 1):
            continue
        if i == 0:
            plane = before_ref[c]
        elif i == plan.planes + 1:
            plane = after_ref[c]
        else:
            plane = x_ref[c, i - 1]
        wide = plane.astype(F32)
        lower = jnp.where(edge == 0, 0.0, pltpu.roll(wide, 1, 0))
        upper = jnp.where(edge == NX - 1, 0.0, pltpu.roll(wide, NX - 1, 0))
        cols = slice(i * NY, (i + 1) * NY)
        rows_ref[0, :, cols] = lower.astype(BF16)
        rows_ref[1, :, cols] = plane
        rows_ref[2, :, cols] = upper.astype(BF16)


def stencil_kernel(plan, batch, adjoint, group, offset, *refs):
    if offset:
        refs = refs[1:]
    if adjoint:
        taps_ref, x_ref, out_ref, band_ref, rows_ref = refs
        before_ref = after_ref = None
    else:
        taps_ref, x_ref, before_ref, after_ref, out_ref, band_ref, rows_ref = refs

    @pl.when(pl.program_id(0) == 0)
    def _():
        band_ref[...] = jnp.zeros_like(band_ref)
        rows_ref[...] = jnp.zeros_like(rows_ref)

    first = pl.program_id(0) * batch + offset
    for c in range(batch):
        half = c % 2
        band, rows = band_ref.at[half], rows_ref.at[half]
        bands(taps_ref, first + c, adjoint, group, band)
        shifted(plan, x_ref, before_ref, after_ref, c, rows)
        for z in range(0, plan.planes, group):
            cols = slice(z * NY, (z + group + 2) * NY)
            near = jnp.concatenate([rows[d, :, cols] for d in range(3)], axis=1)
            total = dot(near, band[...])
            for i in range(group):
                out_ref[c, z + i] = total[:, i * NY : (i + 1) * NY].astype(BF16)


def stencil_call(plan, taps, field, rims, adjoint, done=None):
    channels, planes = field.shape[:2]
    batch = 4
    group = 2 if planes % 2 == 0 else 1
    offset = 0 if done is None else channels // 2
    skip = offset // batch
    block = pl.BlockSpec((batch, planes, NX, NY), lambda i: (i + skip, 0, 0, 0))
    specs = [pl.BlockSpec(memory_space=pltpu.SMEM), block]
    specs += [pl.BlockSpec((batch, NX, NY), lambda i: (i + skip, 0, 0))] * len(rims)
    operands = (taps, field, *rims)
    if done is not None:
        specs = [pl.BlockSpec(memory_space=pl.ANY)] + specs
        operands = (done,) + operands
    return pl.pallas_call(
        functools.partial(stencil_kernel, plan, batch, adjoint, group, offset),
        grid=(channels // 2 // batch,),
        in_specs=specs,
        out_specs=block,
        out_shape=jax.ShapeDtypeStruct(field.shape, BF16),
        input_output_aliases={} if done is None else {0: 0},
        scratch_shapes=[
            pltpu.VMEM((2, 3 * (group + 2) * NY, group * NY), BF16),
            pltpu.VMEM((2, 3, NX, (planes + 2) * NY), BF16),
        ],
        compiler_params=params(60),
        cost_estimate=pl.CostEstimate(
            flops=field.size * 3 * (group + 2) * NY, bytes_accessed=field.size * 2, transcendentals=0
        ),
        name="stencil_back" if adjoint else "stencil",
    )(*operands)


def final_kernel(plan, batch, taps_ref, x_ref, before_ref, after_ref, m_ref, tx_ref, ty_ref, out_ref):
    first = pl.program_id(0) * batch
    edge = lax.broadcasted_iota(jnp.int32, (NX, NY), 0)
    diff = lax.broadcasted_iota(jnp.int32, (NY, NY), 0) - lax.broadcasted_iota(jnp.int32, (NY, NY), 1)

    def rim(c, plane, dz):
        wide = plane.astype(F32)
        lower = jnp.where(edge == 0, 0.0, pltpu.roll(wide, 1, 0)).astype(BF16)
        upper = jnp.where(edge == NX - 1, 0.0, pltpu.roll(wide, NX - 1, 0)).astype(BF16)
        band = []
        for dx in (2, 1, 0):
            t = [taps_ref[9 * dz + 3 * dx + i, first + c] for i in range(3)]
            band.append(jnp.where(
                diff == 0,
                t[1],
                jnp.where(diff == 1, t[0], jnp.where(diff == -1, t[2], 0.0)),
            ).astype(BF16))
        return dot(jnp.concatenate([lower, plane, upper], axis=1), jnp.concatenate(band, axis=0))

    for c in range(batch):
        wave = dot(tx_ref[...], get_modes(plan, m_ref, c)).astype(BF16)
        wave = jnp.concatenate([wave[:NX], wave[NX:]], axis=1)
        full = dot(wave, ty_ref[...])
        for z in range(plan.planes):
            total = full[:, z * NY : (z + 1) * NY] + x_ref[c, z].astype(F32)
            if z == 0:
                total = total + rim(c, before_ref[c], 2)
            if z == plan.planes - 1:
                total = total + rim(c, after_ref[c], 0)
            out_ref[c, z] = total.astype(BF16)


def final_call(plan, taps, partial, before, after, modes, tx, ty):
    channels, planes = partial.shape[:2]
    batch = 4
    block = pl.BlockSpec((batch, planes, NX, NY), lambda i: (i, 0, 0, 0))
    rim = pl.BlockSpec((batch, NX, NY), lambda i: (i, 0, 0))
    return pl.pallas_call(
        functools.partial(final_kernel, plan, batch),
        grid=(channels // batch,),
        in_specs=[
            pl.BlockSpec(memory_space=pltpu.SMEM),
            block,
            rim,
            rim,
            pl.BlockSpec((modes.shape[0], batch) + modes.shape[2:], lambda i: (0, i, 0, 0)),
            whole(tx.shape),
            whole(ty.shape),
        ],
        out_specs=block,
        out_shape=jax.ShapeDtypeStruct(partial.shape, BF16),
        compiler_params=params(60),
        cost_estimate=pl.CostEstimate(
            flops=2 * partial.size * 512, bytes_accessed=partial.size * 4, transcendentals=0
        ),
        name="final",
    )(taps, partial, before, after, modes, tx, ty)


def mix_kernel(plan, channels, adjoint, scale_in, scale_out, r_ref, zf_ref, zi_ref, w_ref,
               out_ref, turned_ref, z_scr, s_scr, m_scr, o_scr):
    jl, lanes, pk, pw = plan.jl, plan.lanes, plan.pk, plan.pw
    chunks = 2 * lanes // 128
    total = None
    for s in range(plan.slabs):
        part = dot(r_ref[s].astype(F32), zf_ref[s], precision=HIGHEST)
        total = part if total is None else total + part
    total = total * scale_in
    for q in range(chunks):
        z_scr[q] = total[:, q * 128 : (q + 1) * 128]

    def rows_of(start):
        return jnp.concatenate(
            [z_scr[q, pl.ds(start, channels, stride=2 * jl), :] for q in range(chunks)], axis=1)

    for j in range(jl):
        re, im = rows_of(j), rows_of(jl + j)
        real = re[:, :lanes] + im[:, lanes:]
        imag = im[:, :lanes] - re[:, lanes:]
        s_scr[j, 0] = real
        s_scr[j, 1] = imag
        both = jnp.concatenate([real, imag], axis=0)
        turned_ref[j * lanes : (j + 1) * lanes, :] = both.T.astype(BF16)
        cols = slice(j * lanes, (j + 1) * lanes)
        rows = slice(j * channels, (j + 1) * channels)
        if adjoint:
            for c in range(channels):
                wr = w_ref[0, c, :, cols].astype(F32)
                wi = w_ref[1, c, :, cols].astype(F32)
                br = jnp.sum(wr * real + wi * imag, axis=0, keepdims=True)
                bi = jnp.sum(wr * imag - wi * real, axis=0, keepdims=True)
                m_scr[j * channels + c : j * channels + c + 1, :lanes] = br
                m_scr[j * channels + c : j * channels + c + 1, lanes:] = bi
        else:
            mr = jnp.zeros((channels, lanes), F32)
            mi = jnp.zeros((channels, lanes), F32)
            for c in range(channels):
                wr = w_ref[0, c, :, cols].astype(F32)
                wi = w_ref[1, c, :, cols].astype(F32)
                sr = s_scr[j, 0, c : c + 1, :]
                si = s_scr[j, 1, c : c + 1, :]
                mr = mr + (sr * wr - si * wi)
                mi = mi + (sr * wi + si * wr)
            m_scr[rows, :lanes] = mr
            m_scr[rows, lanes:] = mi
    mixed = m_scr[...] * scale_out
    for s in range(plan.slabs):
        planar = dot(mixed, zi_ref[s], precision=HIGHEST)
        for j in range(jl):
            for part in range(2):
                o_scr[pl.ds(part * jl + j, channels, stride=2 * jl), :] = planar[
                    j * channels : (j + 1) * channels, part * pw : (part + 1) * pw
                ]
        out_ref[s] = o_scr[:, :pk].astype(BF16)


def mix_call(plan, received, weights, zf, zi, adjoint, scale_in, scale_out):
    channels = weights.shape[1]
    rows = channels * 2 * plan.jl
    modes = plan.jl * plan.lanes
    return pl.pallas_call(
        functools.partial(mix_kernel, plan, channels, adjoint, scale_in, scale_out),
        out_shape=(
            jax.ShapeDtypeStruct((plan.slabs, rows, plan.pk), BF16),
            jax.ShapeDtypeStruct((modes, 2 * channels), BF16),
        ),
        scratch_shapes=[
            pltpu.VMEM((2 * plan.lanes // 128, rows, 128), F32),
            pltpu.VMEM((plan.jl, 2, channels, plan.lanes), F32),
            pltpu.VMEM((plan.jl * channels, 2 * plan.lanes), F32),
            pltpu.VMEM((rows, plan.pw), F32),
        ],
        compiler_params=params(60),
        name="mix_back" if adjoint else "mix",
    )(received, zf, zi, weights)


def middle_kernel(plan, channels, g_ref, sm_ref, cot_ref, m_ref, bias_ref, pw_ref, pt_ref,
                  txi_ref, tyi_ref, ty_ref, tx_ref,
                  spread_ref, first_ref, last_ref, modes_ref, wave_scr, delta_scr, move_scr, kp_ref, kt_ref):
    z = pl.program_id(0)
    planes = plan.planes
    width = plan.width

    @pl.when(z == 0)
    def _():
        def body(c, carry):
            wave = dot(txi_ref[...], get_modes(plan, m_ref, c)).astype(BF16)
            wave_scr[c, :, :width] = wave[:NX]
            wave_scr[c, :, width:] = wave[NX:]
            return carry
        lax.fori_loop(0, channels, body, 0, unroll=4)
        rows = channels * 16
        pick = lax.broadcasted_iota(jnp.int32, (rows, channels), 0) >> 4
        pick = pick == lax.broadcasted_iota(jnp.int32, (rows, channels), 1)
        pick = jnp.where(pick, 1.0, 0.0).astype(BF16)
        same = lax.broadcasted_iota(jnp.int32, (rows, rows), 0) & 15
        same = same == (lax.broadcasted_iota(jnp.int32, (rows, rows), 1) & 15)
        for src, dst in ((pt_ref, kp_ref), (pw_ref, kt_ref)):
            tall = dot(pick, src[...]).astype(BF16)
            full = lax.dot_general(tall, pick, (((1,), (1,)), ((), ())), preferred_element_type=F32)
            dst[...] = jnp.where(same, full, 0.0).astype(BF16)

    g = g_ref[0]
    row = lax.broadcasted_iota(jnp.int32, (NX, NY), 0)
    col = lax.broadcasted_iota(jnp.int32, (NX, NY), 1)

    def differs(shift, axis, inside):
        return jnp.where((g != pltpu.roll(g, shift, axis)) & inside, 0.25, 0.0)

    move_scr[...] = (
        0.25
        + differs(1, 0, row > 0)
        + differs(NX - 1, 0, row < NX - 1)
        + differs(1, 1, col > 0)
        + differs(NY - 1, 1, col < NY - 1)
    )
    height = channels * 16
    bias = bias_ref[...]

    def body(pair, carry):
        starts = [pair * 32 + 16 * i for i in range(2)]

        def tile(ref):
            return [ref[:, 0, pl.ds(x, 16), :].reshape(height, NY) for x in starts]

        mixed = dot(kp_ref[...], jnp.concatenate(tile(sm_ref), axis=1))
        cot = tile(cot_ref)
        deltas = []
        for i, x in enumerate(starts):
            moving = move_scr[pl.ds(x, 16), :]
            wave = wave_scr[:, pl.ds(x, 16), :].reshape(height, 2 * width)
            spectral = dot(wave, tyi_ref[...])
            local = mixed[:, i * NY : (i + 1) * NY].reshape(channels, 16, NY) * moving[None]
            pre = spectral.reshape(channels, 16, NY) + local + bias
            gate = 0.5 + 0.5 * jnp.tanh(0.5 * pre)
            delta = cot[i].astype(F32).reshape(channels, 16, NY) * gate * (1.0 + pre * (1.0 - gate))
            delta = delta.astype(BF16)
            delta_scr[:, z, pl.ds(x, 16), :] = delta
            deltas.append(delta.reshape(height, NY))
        turned = dot(kt_ref[...], jnp.concatenate(deltas, axis=1))
        for i, x in enumerate(starts):
            moving = move_scr[pl.ds(x, 16), :]
            value = turned[:, i * NY : (i + 1) * NY].reshape(channels, 16, NY) * moving[None]
            spread_ref[:, 0, pl.ds(x, 16), :] = value.astype(BF16)
        return carry

    for pair in range(NX // 32):
        body(pair, 0)

    @pl.when(z == 0)
    def _():
        first_ref[...] = spread_ref[:, 0]

    @pl.when(z == planes - 1)
    def _():
        last_ref[...] = spread_ref[:, 0]

        def body(i, carry):
            for c in (2 * i, 2 * i + 1):
                value = channel_modes(plan, lambda p: delta_scr[c, p], ty_ref[...], tx_ref[...])
                put_modes(plan, modes_ref, c, value)
            return carry

        lax.fori_loop(0, channels // 2, body, 0)


def middle_call(plan, grains, smooth, cotangent, modes, bias, kp, kt, txi, tyi, ty, tx):
    channels, planes = smooth.shape[:2]
    width = plan.width
    block = pl.BlockSpec((channels, 1, NX, NY), lambda z: (0, z, 0, 0))
    rim = jax.ShapeDtypeStruct((channels, NX, NY), BF16)
    return pl.pallas_call(
        functools.partial(middle_kernel, plan, channels),
        grid=(planes,),
        in_specs=[
            pl.BlockSpec((1, NX, NY), lambda z: (z, 0, 0)),
            block,
            block,
            whole(modes.shape),
            whole((channels, 1, 1)),
            whole(kp.shape),
            whole(kt.shape),
            whole(txi.shape),
            pl.BlockSpec((2 * width, NY), lambda z: (0, z)),
            whole(ty.shape),
            whole(tx.shape),
        ],
        out_specs=[block, whole(rim.shape), whole(rim.shape), whole(modes.shape)],
        out_shape=[jax.ShapeDtypeStruct(smooth.shape, BF16), rim, rim,
                   jax.ShapeDtypeStruct(modes.shape, BF16)],
        scratch_shapes=[
            pltpu.VMEM((channels, NX, 2 * width), BF16),
            pltpu.VMEM((channels, planes, NX, NY), BF16),
            pltpu.VMEM((NX, NY), F32),
            pltpu.VMEM((16 * channels, 16 * channels), BF16),
            pltpu.VMEM((16 * channels, 16 * channels), BF16),
        ],
        compiler_params=params(60),
        name="middle",
    )(grains, smooth, cotangent, modes, bias.reshape(channels, 1, 1), kp, kt, txi, tyi, ty, tx)


def grad_kernel(samples, both_ref, e_ref, out_ref):
    total = None
    for i in range(samples):
        half = both_ref.shape[-1] // 2
        spec, dual = both_ref[i, :, :half], both_ref[i, :, half:]
        term = dot(spec, e_ref[0]) * dot(dual, e_ref[1]) + dot(spec, e_ref[2]) * dot(dual, e_ref[3])
        total = term if total is None else total + term
    out_ref[...] = total


def grad_call(both, pick):
    samples, modes, width = both.shape
    columns = pick.shape[-1]
    batch = min(256, modes)
    return pl.pallas_call(
        functools.partial(grad_kernel, samples),
        grid=(modes // batch,),
        in_specs=[
            pl.BlockSpec((samples, batch, width), lambda i: (0, i, 0)),
            whole(pick.shape),
        ],
        out_specs=pl.BlockSpec((batch, columns), lambda i: (i, 0)),
        out_shape=jax.ShapeDtypeStruct((modes, columns), F32),
        compiler_params=params(60),
        cost_estimate=pl.CostEstimate(
            flops=8 * samples * modes * width * columns, bytes_accessed=modes * columns * 4, transcendentals=0
        ),
        name="grad_modes",
    )(both, pick)


def column_picks(channels, columns):
    column = lax.axis_index("dp") * columns + jnp.arange(columns)
    part = column // (channels * channels)
    c = column // channels % channels
    o = column % channels
    index = jnp.arange(2 * channels)[:, None]
    spec_real = (index == c).astype(F32)
    spec_imag = (index == channels + c).astype(F32) * jnp.where(part == 0, 1.0, -1.0)
    dual_same = (index == part * channels + o).astype(F32)
    dual_other = (index == (1 - part) * channels + o).astype(F32)
    return jnp.stack([spec_real, dual_same, spec_imag, dual_other]).astype(BF16)


def local(feats, grains, spec_weight, taps, point_weight, bias, cotangent):
    samples_here, channels, planes = feats.shape[:3]
    assert samples_here == 1
    slabs = lax.axis_size("slab")
    dp = lax.axis_size("dp")
    plan = Plan(planes, slabs)
    mode_rows = spec_weight.shape[0]
    half = lambda t: jnp.asarray(t.astype(jnp.bfloat16))
    ty, tx = half(plan.y_forward), half(plan.x_forward)
    tyi, txi = half(plan.y_inverse), half(plan.x_inverse)
    zf = jnp.asarray(plan.z_forward.astype(np.float32))
    zi = jnp.asarray(plan.z_inverse.astype(np.float32))
    cell_scale = 1.0 / math.sqrt(NX * NY * NZ)
    mode_scale = 1.0 / math.sqrt(KX * KY * KZ)
    jl, kq, kk, groups = plan.jl, plan.kq, plan.kk, plan.groups

    def swap(value):
        return lax.all_to_all(value, "slab", split_axis=0, concat_axis=0, tiled=True)

    def scatter_modes(modes):
        if plan.lead == 1 or kq > 1 or plan.used < plan.width:
            modes = modes[..., : plan.used].reshape(plan.lead, channels, -1, 2 * jl, planes, kq, kk)
            modes = modes.transpose(0, 2, 5, 1, 3, 4, 6)
        return swap(modes.reshape(slabs, channels * 2 * jl, plan.pk))

    def gather_planes(planar):
        planar = swap(planar)
        if plan.lead == 1 or kq > 1 or plan.used < plan.width:
            planar = planar.reshape(plan.lead, groups // plan.lead, kq, channels, 2 * jl, planes, kk)
            planar = planar.transpose(0, 3, 1, 4, 5, 2, 6).reshape(
                plan.lead, channels, 2 * KX // plan.lead, plan.used)
            return jnp.pad(planar, ((0, 0), (0, 0), (0, 0), (0, plan.width - plan.used)))
        return planar.reshape(plan.lead, channels, 2 * KX // plan.lead, plan.width)

    up = [(i, i + 1) for i in range(slabs - 1)]
    down = [(j, i) for i, j in up]
    field = feats[0]
    low, high = rims_call(field)
    before = lax.ppermute(high, "slab", up)
    after = lax.ppermute(low, "slab", down)
    weights = spec_weight.reshape(mode_rows * KZ, 2 * channels * channels).T
    weights = weights.reshape(2, channels, channels, mode_rows * KZ)
    kp, kt = point_weight, point_weight.T

    received = scatter_modes(planes_call(plan, field, ty, tx))
    smooth = stencil_call(plan, taps, field, (before, after), False)
    received, smooth = lax.optimization_barrier((received, smooth))
    mixed, spec = mix_call(plan, received, weights, zf, zi, False, cell_scale, mode_scale)
    mixed, smooth = lax.optimization_barrier((mixed, smooth))
    modes = gather_planes(mixed)
    smooth = stencil_call(plan, taps, field, (before, after), False, smooth)
    spread, first, last, dual_modes = middle_call(
        plan, grains[0], smooth, cotangent[0], modes, bias, kp, kt, txi, tyi, ty, tx)
    spread_before = lax.ppermute(last, "slab", up)
    spread_after = lax.ppermute(first, "slab", down)
    received = scatter_modes(dual_modes)
    partial = stencil_call(plan, taps, spread, (), True)
    received, partial = lax.optimization_barrier((received, partial))
    back, dual = mix_call(plan, received, weights, zf, zi, True, mode_scale, cell_scale)
    back, partial = lax.optimization_barrier((back, partial))
    back_modes = gather_planes(back)
    partial = stencil_call(plan, taps, spread, (), True, partial)
    both = jnp.concatenate([spec, dual], axis=1)
    both = lax.all_to_all(
        jnp.broadcast_to(both[None], (dp,) + both.shape), "dp", split_axis=0, concat_axis=0, tiled=True)
    columns = 2 * channels * channels // dp
    pick = column_picks(channels, columns)
    scale = 1.0 / (samples_here * dp)
    grad_spec = grad_call(both, pick * jnp.array([scale, 1, scale, 1], BF16)[:, None, None])
    grad_feats = final_call(plan, taps, partial, spread_before, spread_after, back_modes, txi, tyi)
    return grad_feats[None], grad_spec.reshape(mode_rows, KZ, columns)


def solution(mesh):
    in_specs = (
        P(("grp", "dp"), None, "slab", None, None),
        P(("grp", "dp"), "slab", None, None),
        P("slab", None, None),
        P(),
        P(),
        P(),
        P(("grp", "dp"), None, "slab", None, None),
    )
    out_specs = (P(("grp", "dp"), None, "slab", None, None), P("slab", "grp", "dp"))
    return jax.shard_map(local, mesh=mesh, in_specs=in_specs, out_specs=out_specs, check_vma=False)
```
